512 devices in a mesh: row: 16 (over x, z_hi, core), col: 32 (over y, z_lo).
Axes of the slice: x: 4, y: 8, z: 8 (z_hi: 2, z_lo: 4; z = z_hi * 4 + z_lo), core: 2. Of those that a mesh axis runs over, the one named last changes fastest.
Arguments:
- first_alignment_matrix: float32 [64, 512, 32], P('row', 'col'), may hold values from -6 to 6
- second_alignment_matrix: float32 [64, 512, 32], P('row', 'col'), may hold values from -6 to 6
- couple_delta_sensitivity: float32 [512, 512, 128], P('row', 'col'), may hold values from -6 to 6
- mapping_matrix: float32 [1024, 128], replicated, may hold values from -0.1875 to 0.1875
Outputs:
- grad_left: float32 [64, 512, 32], P('row', 'col')
- grad_right: float32 [64, 512, 32], P('row', 'col')
The draws below stay inside these ranges and needn't reach their ends.
All inputs are finite; a program needn't handle non-finite values.
Results may differ from the reference program's by a relative error of at most 0.0003.
Values sent between devices are 32-bit elements; how exact they have to be, the bound alone decides.
No kernel may reach another device: no remote copies, remote signals or barrier semaphores. Data moves between devices by JAX's collectives and lax.ppermute only.
A program may use at most 64 MiB of HBM per device.

```python
import jax
import jax.numpy as jnp
from jax import lax

FIRST_FEATURES = 32
SECOND_FEATURES = 32
P_SIZE = 128
RES_DEV = 16
ALIGNED_SEQS = 64
AMINO_TOTAL = 512
N_COL = 32


def block_scale(stream_key, dims, shards, smallest, top_value):
    def one(position, shards_of):
        draws = jax.random.uniform(jax.random.fold_in(jax.random.fold_in(stream_key, 6), position), (shards_of,), jnp.float32, smallest / len(shards), top_value / len(shards))
        return jnp.repeat(jnp.exp(draws), dims[position] // shards_of).reshape((-1,) + (1,) * (len(dims) - position - 1))

    gain = one(*shards[0])
    for cut in shards[1:]:
        gain = gain * one(*cut)
    return gain


def noise(stream_key, extent, width, limit, cuts=(), held_as=jnp.bfloat16):
    values = width * jax.random.normal(stream_key, extent, jnp.float32)
    if cuts:
        values = values * block_scale(stream_key, extent, cuts, -0.22, 0.18)
    return jnp.clip(values, -limit, limit).astype(held_as)


def setup_inputs(seed: int = 0) -> dict:
    keys = jax.random.split(jax.random.key(seed), 5)
    return {
        "first_alignment_matrix": noise(keys[0], (ALIGNED_SEQS, AMINO_TOTAL, FIRST_FEATURES), 1.0, 6.0, ((0, 16), (1, 32)), jnp.float32),
        "second_alignment_matrix": noise(keys[1], (ALIGNED_SEQS, AMINO_TOTAL, SECOND_FEATURES), 1.0, 6.0, ((0, 16), (1, 32)), jnp.float32),
        "couple_delta_sensitivity": noise(keys[2], (AMINO_TOTAL, AMINO_TOTAL, P_SIZE), 1.0, 6.0, ((0, 16), (1, 32)), jnp.float32),
        "mapping_matrix": noise(keys[3], (FIRST_FEATURES * SECOND_FEATURES, P_SIZE), (FIRST_FEATURES * SECOND_FEATURES) ** -0.5, 0.1875, (), jnp.float32),
    }


def reference(first_alignment_matrix, second_alignment_matrix, couple_delta_sensitivity, mapping_matrix):
    exact_arithmetic = lax.Precision.HIGHEST
    summed_extent = first_alignment_matrix.shape[0]
    weight3 = mapping_matrix.reshape(FIRST_FEATURES, SECOND_FEATURES, P_SIZE)

    def left_block(index):
        start = (index * RES_DEV).astype(jnp.int32)
        amino_block = lax.dynamic_slice_in_dim(couple_delta_sensitivity, start, RES_DEV, 0)
        dotted_result = jnp.einsum('hiw,gic->hgwc', amino_block, second_alignment_matrix, precision=exact_arithmetic)
        return jnp.einsum('ispe,cep->sic', dotted_result, weight3, precision=exact_arithmetic) / summed_extent

    def right_block(index):
        start = (index * RES_DEV).astype(jnp.int32)
        amino_block = lax.dynamic_slice_in_dim(couple_delta_sensitivity, start, RES_DEV, 1)
        dotted_result = jnp.einsum('gdl,pgv->dplv', amino_block, first_alignment_matrix, precision=exact_arithmetic)
        return jnp.einsum('jspc,cep->sje', dotted_result, weight3, precision=exact_arithmetic) / summed_extent

    steps = jnp.arange(N_COL, dtype=jnp.int32)
    left_parts = lax.map(left_block, steps)
    right_parts = lax.map(right_block, steps)
    grad_left = jnp.transpose(left_parts, (1, 0, 2, 3)).reshape(summed_extent, AMINO_TOTAL, FIRST_FEATURES)
    grad_right = jnp.transpose(right_parts, (1, 0, 2, 3)).reshape(summed_extent, AMINO_TOTAL, SECOND_FEATURES)
    return (grad_left, grad_right)
```

```python
import jax
import jax.numpy as jnp
from jax import lax
from jax.sharding import PartitionSpec as P

LANES = 128


def swap_pairs(rows, cols):
    half = cols // rows
    return [
        (r * cols + c, (c // half) * cols + half * r + c % half)
        for r in range(rows)
        for c in range(cols)
    ]


def to_all(block, axis):
    count = lax.axis_size(axis)
    spread = jnp.broadcast_to(block[None], (count,) + block.shape)
    return lax.all_to_all(spread, axis, split_axis=0, concat_axis=0, tiled=True)


def sum_to_owner(chunks, axis):
    moved = lax.all_to_all(chunks, axis, split_axis=0, concat_axis=0, tiled=True)
    return moved.sum(axis=0)


def on_device(left, right, grad, mapping):
    exact = lax.Precision.HIGH
    rows, cols = lax.axis_size("row"), lax.axis_size("col")
    half = cols // rows
    seqs, res, feat_c = left.shape
    feat_e = right.shape[2]
    tile_i, tile_j, pair = grad.shape
    total = seqs * rows
    pairs = swap_pairs(rows, cols)

    left_moved = lax.ppermute(left.reshape(-1, LANES), ("row", "col"), pairs)
    right_all = to_all(right.reshape(-1, LANES), "row")
    left_all = to_all(left_moved, "col")
    right_flat = right_all.reshape(total, tile_j * feat_e)
    left_flat = left_all.reshape(rows, half, seqs, res, feat_c).transpose(0, 2, 1, 3, 4)
    left_flat = left_flat.reshape(total, tile_i * feat_c)

    weight3 = mapping.reshape(feat_c, feat_e, pair)
    outer = jnp.einsum("ijp,cep->icje", grad, weight3, precision=exact)
    outer = outer.reshape(tile_i * feat_c, tile_j * feat_e)
    left_part = jnp.einsum("sk,xk->sx", right_flat, outer, precision=exact) / total
    right_part = jnp.einsum("sx,xk->sk", left_flat, outer, precision=exact) / total

    chunks = left_part.reshape(rows, seqs, half, res, feat_c).transpose(0, 2, 1, 3, 4)
    left_sum = sum_to_owner(chunks.reshape(cols, -1, LANES), "col")
    grad_left = lax.ppermute(left_sum, ("row", "col"), pairs).reshape(left.shape)
    grad_right = sum_to_owner(right_part.reshape(rows, -1, LANES), "row").reshape(right.shape)
    return (grad_left, grad_right)


def solution(mesh):
    spec = P("row", "col", None)
    return jax.shard_map(
        on_device,
        mesh=mesh,
        in_specs=(spec, spec, spec, P()),
        out_specs=(spec, spec),
        check_vma=False,
    )
```

```python
import jax
import jax.numpy as jnp
from jax import lax
from jax.experimental import pallas as pl
from jax.experimental.pallas import tpu as pltpu
from jax.sharding import PartitionSpec as P

LANES = 128
NT = (((1,), (1,)), ((), ()))
NN = (((1,), (0,)), ((), ()))


def split(x):
    high = x.astype(jnp.bfloat16)
    return high, (x - high.astype(jnp.float32)).astype(jnp.bfloat16)


def product(a, b, dims):
    return lax.dot_general(a, b, dims, preferred_element_type=jnp.float32)


def swap_lane_groups(x, width):
    lane = lax.broadcasted_iota(jnp.int32, x[0].shape, 1)
    count, step = len(x), len(x) // 2
    while step:
        first = (lane // (width * step)) % 2 == 0
        y = list(x)
        for j in range(count):
            if (j // step) % 2 == 0:
                a, b, shift = x[j], x[j + step], width * step
                y[j] = jnp.where(first, a, pltpu.roll(b, shift, 1))
                y[j + step] = jnp.where(first, pltpu.roll(a, LANES - shift, 1), b)
        x, step = y, step // 2
    return x


def outer_kernel(tile_i, tile_j, feat_e, grad_ref, map_ref, high_ref, low_ref):
    group = LANES // feat_e
    part = tile_i // 2
    block = 2 * LANES
    rows = high_ref.shape[0] // 2
    grad = jnp.concatenate(
        [grad_ref[pl.ds(j, tile_i, stride=tile_j), :] for j in range(tile_j)], axis=0
    )
    grad_high, grad_low = split(grad)
    grad_both = jnp.concatenate([grad_high, grad_low], axis=1)
    for n in range(map_ref.shape[0] // block):
        map_high, map_low = split(map_ref[n * block : (n + 1) * block, :])
        map_both = jnp.concatenate([map_high, map_high], axis=1)
        full = product(grad_both, map_both, NT) + product(grad_high, map_low, NT)
        for m in range(block // LANES):
            for g in range(tile_j // group):
                tiles = [
                    full[(g * group + j) * tile_i :][:tile_i, m * LANES : (m + 1) * LANES]
                    for j in range(group)
                ]
                for k, tile in enumerate(swap_lane_groups(tiles, feat_e)):
                    channel = (n * (block // LANES) + m) * group + k
                    high, low = split(tile)
                    for h in range(2):
                        row = pl.ds(h * rows + channel * part, part)
                        lanes = pl.ds(g * LANES, LANES)
                        high_ref[row, lanes] = high[h * part : (h + 1) * part]
                        low_ref[row, lanes] = low[h * part : (h + 1) * part]


def load_rows(ref, first, total, pieces):
    return jnp.concatenate(
        [ref[pl.ds(first + p, total, stride=pieces), :] for p in range(pieces)], axis=1
    )


def left_kernel(total, gathered_ref, high_ref, low_ref, out_ref):
    pieces = gathered_ref.shape[0] // total
    b_high, b_low = split(load_rows(gathered_ref, 0, total, pieces))
    both = product(jnp.concatenate([b_high, b_low], axis=0), high_ref[...], NT)
    left = both[:total] + both[total:] + product(b_high, low_ref[...], NT)
    left = left * (1.0 / total)
    pieces = out_ref.shape[0] // (2 * total)
    for h in range(2):
        for p in range(pieces):
            at = (h * pieces + p) * LANES
            out_ref[pl.ds(h * total * pieces + p, total, stride=pieces), :] = left[:, at : at + LANES]


def right_kernel(total, gathered_ref, high_ref, low_ref, out_ref):
    pieces = gathered_ref.shape[0] // (2 * total)
    a_full = jnp.concatenate(
        [load_rows(gathered_ref, h * total * pieces, total, pieces) for h in range(2)], axis=1
    )
    a_high, a_low = split(a_full)
    both = product(jnp.concatenate([a_high, a_low], axis=0), high_ref[...], NN)
    right = both[:total] + both[total:] + product(a_high, low_ref[...], NN)
    right = right * (1.0 / total)
    pieces = out_ref.shape[0] // total
    for p in range(pieces):
        out_ref[pl.ds(p, total, stride=pieces), :] = right[:, p * LANES : (p + 1) * LANES]


def outer_parts(grad, mapping, feat_c, feat_e, interpret=False):
    import functools
    tile_i, tile_j, pair = grad.shape
    shape = jax.ShapeDtypeStruct((tile_i * feat_c, tile_j * feat_e), jnp.bfloat16)
    return pl.pallas_call(
        functools.partial(outer_kernel, tile_i, tile_j, feat_e),
        out_shape=(shape, shape), interpret=interpret, name="outer",
    )(grad.reshape(tile_i * tile_j, pair), mapping)


def contract(kernel, name, total, gathered, parts, rows, interpret=False):
    import functools
    return pl.pallas_call(
        functools.partial(kernel, total),
        out_shape=jax.ShapeDtypeStruct((rows, LANES), jnp.float32), interpret=interpret, name=name,
    )(gathered, *parts)


def pair_moves(rows, cols):
    half = cols // rows
    return [
        (r * cols + c, (c // half) * cols + (c % half) * rows + r)
        for r in range(rows)
        for c in range(cols)
    ]


def to_all(block, axis):
    count = lax.axis_size(axis)
    spread = jnp.broadcast_to(block[None], (count,) + block.shape)
    return lax.all_to_all(spread, axis, split_axis=0, concat_axis=0, tiled=True)


def sum_to_owner(chunks, axis):
    chunks = chunks.reshape(lax.axis_size(axis), -1, LANES)
    moved = lax.all_to_all(chunks, axis, split_axis=0, concat_axis=0, tiled=True)
    return moved.sum(axis=0)


def on_device(left, right, grad, mapping):
    rows, cols = lax.axis_size("row"), lax.axis_size("col")
    seqs, res, feat_c = left.shape
    feat_e = right.shape[2]
    total = seqs * rows
    moves = pair_moves(rows, cols)
    back = [(b, a) for a, b in moves]
    both = ("row", "col")

    left_block = left.transpose(0, 2, 1).reshape(-1, LANES)
    right_block = right.reshape(-1, LANES)
    left_all = to_all(lax.ppermute(left_block, both, moves), "col").reshape(-1, LANES)
    right_all = to_all(right_block, "row").reshape(-1, LANES)
    parts = outer_parts(grad, mapping, feat_c, feat_e)
    left_part = contract(left_kernel, "left", total, right_all, parts, left_all.shape[0])
    left_sum = lax.ppermute(sum_to_owner(left_part, "col"), both, back)
    right_part = contract(right_kernel, "right", total, left_all, parts, right_all.shape[0])
    right_sum = sum_to_owner(right_part, "row")
    grad_left = left_sum.reshape(seqs, feat_c, res).transpose(0, 2, 1)
    return (grad_left, right_sum.reshape(right.shape))


def solution(mesh):
    spec = P("row", "col", None)
    return jax.shard_map(
        on_device,
        mesh=mesh,
        in_specs=(spec, spec, spec, P()),
        out_specs=(spec, spec),
        check_vma=False,
    )
```

```python
import functools

import jax
import jax.numpy as jnp
from jax import lax
from jax.experimental import pallas as pl
from jax.experimental.pallas import tpu as pltpu
from jax.sharding import PartitionSpec as P

LANES = 128
NT = (((1,), (1,)), ((), ()))
NN = (((1,), (0,)), ((), ()))


def split(x):
    high = x.astype(jnp.bfloat16)
    return high, (x - high.astype(jnp.float32)).astype(jnp.bfloat16)


def product(a, b, dims):
    return lax.dot_general(a, b, dims, preferred_element_type=jnp.float32)


def swap_lane_groups(x, width):
    lane = lax.broadcasted_iota(jnp.int32, x[0].shape, 1)
    count, step = len(x), len(x) // 2
    while step:
        first = (lane // (width * step)) % 2 == 0
        y = list(x)
        for j in range(count):
            if (j // step) % 2 == 0:
                a, b, shift = x[j], x[j + step], width * step
                y[j] = jnp.where(first, a, pltpu.roll(b, shift, 1))
                y[j + step] = jnp.where(first, pltpu.roll(a, LANES - shift, 1), b)
        x, step = y, step // 2
    return x


def outer_kernel(tile_i, tile_j, feat_e, grad_ref, map_ref, high_ref, low_ref):
    group = LANES // feat_e
    part = tile_i // 2
    block = 2 * LANES
    rows = high_ref.shape[0] // 2
    grad = jnp.concatenate(
        [grad_ref[pl.ds(j, tile_i, stride=tile_j), :] for j in range(tile_j)], axis=0
    )
    grad_high, grad_low = split(grad)
    grad_both = jnp.concatenate([grad_high, grad_low], axis=1)
    for n in range(map_ref.shape[0] // block):
        map_high, map_low = split(map_ref[n * block : (n + 1) * block, :])
        map_both = jnp.concatenate([map_high, map_high], axis=1)
        full = product(grad_both, map_both, NT) + product(grad_high, map_low, NT)
        for m in range(block // LANES):
            for g in range(tile_j // group):
                tiles = [
                    full[(g * group + j) * tile_i :][:tile_i, m * LANES : (m + 1) * LANES]
                    for j in range(group)
                ]
                for k, tile in enumerate(swap_lane_groups(tiles, feat_e)):
                    channel = (n * (block // LANES) + m) * group + k
                    high, low = split(tile)
                    for h in range(2):
                        row = pl.ds(h * rows + channel * part, part)
                        lanes = pl.ds(g * LANES, LANES)
                        high_ref[row, lanes] = high[h * part : (h + 1) * part]
                        low_ref[row, lanes] = low[h * part : (h + 1) * part]


def load_rows(ref, first, total, pieces):
    return jnp.concatenate(
        [ref[pl.ds(first + p, total, stride=pieces), :] for p in range(pieces)], axis=1
    )


def left_kernel(total, gathered_ref, block_ref, high_ref, low_ref, out_ref):
    pieces = gathered_ref.shape[0] // total
    b_high, b_low = split(load_rows(gathered_ref, 0, total, pieces))
    both = product(jnp.concatenate([b_high, b_low], axis=0), high_ref[...], NT)
    left = both[:total] + both[total:] + product(b_high, low_ref[...], NT)
    left = left * (1.0 / total)
    turn = out_ref.shape[0] // (2 * total)
    pieces = turn // 2
    seqs = block_ref.shape[0] // pieces
    for p in range(pieces):
        mine = block_ref[pl.ds(p, seqs, stride=pieces), :]
        mine = jnp.concatenate([mine] * (total // seqs), axis=0)
        for h in range(2):
            lanes = (h * pieces + p) * LANES
            row = h * total * turn + p
            out_ref[pl.ds(row, total, stride=turn), :] = mine
            out_ref[pl.ds(row + pieces, total, stride=turn), :] = left[:, lanes : lanes + LANES]


def right_kernel(total, seqs, gathered_ref, high_ref, low_ref, out_ref, sum_ref):
    turn = gathered_ref.shape[0] // (2 * total)
    pieces = turn // 2
    a_full = jnp.concatenate(
        [
            gathered_ref[pl.ds(h * total * turn + p, total, stride=turn), :]
            for h in range(2)
            for p in range(pieces)
        ],
        axis=1,
    )
    a_high, a_low = split(a_full)
    both = product(jnp.concatenate([a_high, a_low], axis=0), high_ref[...], NN)
    right = both[:total] + both[total:] + product(a_high, low_ref[...], NN)
    right = right * (1.0 / total)
    block = seqs * turn
    chunks = [gathered_ref[k : k + block, :] for k in range(0, gathered_ref.shape[0], block)]
    while len(chunks) > 1:
        chunks = [a + b for a, b in zip(chunks[::2], chunks[1::2])]
    for s in range(seqs):
        sum_ref[s * pieces : (s + 1) * pieces, :] = chunks[0][s * turn + pieces : (s + 1) * turn]
    pieces = out_ref.shape[0] // total
    for p in range(pieces):
        out_ref[pl.ds(p, total, stride=pieces), :] = right[:, p * LANES : (p + 1) * LANES]


VMEM = pl.BlockSpec(memory_space=pltpu.VMEM)


def call(kernel, name, outs, *args, interpret=False):
    return pl.pallas_call(
        kernel,
        out_shape=tuple(jax.ShapeDtypeStruct(shape, dtype) for shape, dtype in outs),
        in_specs=[VMEM] * len(args),
        out_specs=(VMEM,) * len(outs),
        interpret=interpret,
        name=name,
    )(*args)


def pair_moves(rows, cols):
    half = cols // rows
    return [
        (r * cols + c, (c // half) * cols + (c % half) * rows + r)
        for r in range(rows)
        for c in range(cols)
    ]


def to_each(chunks, axis):
    chunks = chunks.reshape(lax.axis_size(axis), -1, LANES)
    return lax.all_to_all(chunks, axis, split_axis=0, concat_axis=0, tiled=True)


def on_device(left, right, grad, mapping, interpret=False):
    rows, cols = lax.axis_size("row"), lax.axis_size("col")
    seqs, res, feat_c = left.shape
    feat_e = right.shape[2]
    tile_i, tile_j, pair = grad.shape
    total = seqs * rows
    f32, bf16 = jnp.float32, jnp.bfloat16
    run = functools.partial(call, interpret=interpret)
    moves = pair_moves(rows, cols)
    back = [(b, a) for a, b in moves]
    both = ("row", "col")

    left_block = lax.ppermute(left.transpose(0, 2, 1).reshape(-1, LANES), both, moves)
    right_block = right.reshape(-1, LANES)
    right_all = to_each(jnp.broadcast_to(right_block[None], (rows,) + right_block.shape), "row")
    outer_shape = (tile_i * feat_c, tile_j * feat_e)
    high, low = run(
        functools.partial(outer_kernel, tile_i, tile_j, feat_e), "outer",
        [(outer_shape, bf16)] * 2, grad.reshape(tile_i * tile_j, pair), mapping,
    )
    block_rows = left_block.shape[0]
    (shared,) = run(
        functools.partial(left_kernel, total), "left", [((cols * 2 * block_rows, LANES), f32)],
        right_all.reshape(-1, LANES), left_block, high, low,
    )
    shared = to_each(shared, "col").reshape(-1, LANES)
    right_part, left_sum = run(
        functools.partial(right_kernel, total, seqs), "right",
        [((rows * right_block.shape[0], LANES), f32), (left_block.shape, f32)], shared, high, low,
    )
    left_sum = lax.ppermute(left_sum, both, back)
    right_sum = to_each(right_part, "row").sum(axis=0)
    grad_left = left_sum.reshape(seqs, feat_c, res).transpose(0, 2, 1)
    return (grad_left, right_sum.reshape(right.shape))


def solution(mesh):
    spec = P("row", "col", None)
    return jax.shard_map(
        on_device,
        mesh=mesh,
        in_specs=(spec, spec, spec, P()),
        out_specs=(spec, spec),
        check_vma=False,
    )
```

```python
import functools

import jax
import jax.numpy as jnp
from jax import lax
from jax.experimental import pallas as pl
from jax.experimental.pallas import tpu as pltpu
from jax.sharding import PartitionSpec as P

LANES = 128
NT = (((1,), (1,)), ((), ()))
NN = (((1,), (0,)), ((), ()))


def split(x):
    high = x.astype(jnp.bfloat16)
    return high, (x - high.astype(jnp.float32)).astype(jnp.bfloat16)


def product(a, b, dims):
    return lax.dot_general(a, b, dims, preferred_element_type=jnp.float32)


def swap_lane_groups(x):
    width = LANES // 4
    place = lax.broadcasted_iota(jnp.int32, x[0].shape, 1) // width
    front, even = place < 2, place % 2 == 0
    cross = (place == 0) | (place == 3)
    pick = jnp.where
    kept = pick(cross, x[0], x[2])
    turned = pltpu.roll(pick(cross, x[2], x[0]), 2 * width, 1)
    other = pltpu.roll(pick(front, x[3], x[1]), 2 * width, 1)
    firsts = (pick(front, kept, turned), pick(front, turned, kept))
    seconds = (pick(front, x[1], other), pick(front, other, x[3]))
    y = []
    for first, second in zip(firsts, seconds):
        turned = pltpu.roll(pick(even, second, first), width, 1)
        y += [pick(even, first, turned), pick(even, turned, second)]
    return y


def outer_kernel(
    tile_i, tile_j, feat_e, grad_hbm, map_hbm, out_ref, grad_ref, map_ref, in_sem
):
    group = LANES // feat_e
    part = tile_i // 2
    block = 2 * LANES
    steps = map_ref.shape[0] // block
    rows = out_ref.shape[0] // 4
    moved = [
        pltpu.make_async_copy(grad_hbm, grad_ref, in_sem.at[0]),
        pltpu.make_async_copy(map_hbm, map_ref, in_sem.at[1]),
    ]
    for copy in moved:
        copy.start()
    for copy in moved:
        copy.wait()
    grads = []
    for g in range(tile_j // group):
        grad = [grad_ref[pl.ds(g * group + j, tile_i, stride=tile_j), :] for j in range(group)]
        high, low = split(jnp.concatenate(grad, axis=0))
        grads.append((high, jnp.concatenate([high, low], axis=1)))
    for n in range(steps):
        map_high, map_low = split(map_ref[n * block : (n + 1) * block, :])
        map_both = jnp.concatenate([map_high, map_high], axis=1)
        for g, (grad_high, grad_both) in enumerate(grads):
            full = product(grad_both, map_both, NT) + product(grad_high, map_low, NT)
            for m in range(block // LANES):
                tiles = [
                    full[j * tile_i : (j + 1) * tile_i, m * LANES : (m + 1) * LANES]
                    for j in range(group)
                ]
                for k, tile in enumerate(swap_lane_groups(tiles)):
                    channel = (n * (block // LANES) + m) * group + k
                    for w, value in enumerate(split(tile)):
                        for h in range(2):
                            row = pl.ds((2 * w + h) * rows + channel * part, part)
                            lanes = pl.ds(g * LANES, LANES)
                            out_ref[row, lanes] = value[h * part : (h + 1) * part]


def load_rows(ref, first, total, pieces):
    return jnp.concatenate(
        [ref[pl.ds(first + p, total, stride=pieces), :] for p in range(pieces)], axis=1
    )


def left_kernel(total, gathered_ref, block_ref, outer_ref, out_ref):
    steps = 4
    pieces = gathered_ref.shape[0] // total
    b_high, b_low = split(load_rows(gathered_ref, 0, total, pieces))
    b_both = jnp.concatenate([b_high, b_low], axis=0)
    turn = out_ref.shape[0] // (2 * total)
    pieces = turn // 2
    seqs = block_ref.shape[0] // pieces
    for p in range(pieces):
        mine = block_ref[pl.ds(p, seqs, stride=pieces), :]
        mine = jnp.concatenate([mine] * (total // seqs), axis=0)
        for h in range(2):
            out_ref[pl.ds(h * total * turn + p, total, stride=turn), :] = mine
    rows = outer_ref.shape[0] // 2
    span = rows // steps
    for n in range(steps):
        both = product(b_both, outer_ref[pl.ds(n * span, span), :], NT)
        last = product(b_high, outer_ref[pl.ds(rows + n * span, span), :], NT)
        left = both[:total] + both[total:] + last
        left = left * (1.0 / total)
        for m in range(span // LANES):
            h, p = divmod(n * (span // LANES) + m, pieces)
            row = h * total * turn + pieces + p
            out_ref[pl.ds(row, total, stride=turn), :] = left[:, m * LANES : (m + 1) * LANES]


def right_kernel(total, seqs, gathered_ref, outer_ref, out_ref, sum_ref):
    turn = gathered_ref.shape[0] // (2 * total)
    pieces = turn // 2
    a_full = jnp.concatenate(
        [
            gathered_ref[pl.ds(h * total * turn + p, total, stride=turn), :]
            for h in range(2)
            for p in range(pieces)
        ],
        axis=1,
    )
    a_high, a_low = split(a_full)
    rows = outer_ref.shape[0] // 2
    both = product(jnp.concatenate([a_high, a_low], axis=0), outer_ref[:rows, :], NN)
    right = both[:total] + both[total:] + product(a_high, outer_ref[rows:, :], NN)
    right = right * (1.0 / total)
    block = seqs * turn
    chunks = [gathered_ref[k : k + block, :] for k in range(0, gathered_ref.shape[0], block)]
    while len(chunks) > 1:
        chunks = [a + b for a, b in zip(chunks[::2], chunks[1::2])]
    for s in range(seqs):
        sum_ref[s * pieces : (s + 1) * pieces, :] = chunks[0][s * turn + pieces : (s + 1) * turn]
    pieces = out_ref.shape[0] // total
    for p in range(pieces):
        out_ref[pl.ds(p, total, stride=pieces), :] = right[:, p * LANES : (p + 1) * LANES]


def pack_kernel(feat_c, feat_e, left_ref, right_ref, block_ref, spread_ref, flat_ref):
    count = block_ref.shape[0]
    group = LANES // feat_e
    pieces = [right_ref[pl.ds(g, count, stride=group), :] for g in range(group)]
    mine = jnp.concatenate(pieces, axis=1)
    for k in range(spread_ref.shape[0] // count):
        spread_ref[k * count : (k + 1) * count, :] = mine
    res = LANES * count // flat_ref.shape[0]
    for s in range(left_ref.shape[0] // res):
        flat_ref[s * feat_c : (s + 1) * feat_c, :] = left_ref[s * res : (s + 1) * res, :].T
    group = LANES // res
    pieces = [flat_ref[pl.ds(g, count, stride=group), :] for g in range(group)]
    block_ref[...] = jnp.concatenate(pieces, axis=1)


def unpack_kernel(feat_c, feat_e, sum_ref, parts_ref, left_ref, right_ref, flat_ref):
    count = sum_ref.shape[0]
    res = LANES * count // flat_ref.shape[0]
    group = LANES // res
    for g in range(group):
        flat_ref[pl.ds(g, count, stride=group), :] = sum_ref[:, g * res : (g + 1) * res]
    for s in range(left_ref.shape[0] // res):
        left_ref[s * res : (s + 1) * res, :] = flat_ref[s * feat_c : (s + 1) * feat_c, :].T
    parts = [parts_ref[k : k + count, :] for k in range(0, parts_ref.shape[0], count)]
    while len(parts) > 1:
        parts = [a + b for a, b in zip(parts[::2], parts[1::2])]
    group = LANES // feat_e
    for g in range(group):
        right_ref[pl.ds(g, count, stride=group), :] = parts[0][:, g * feat_e : (g + 1) * feat_e]


VMEM = pl.BlockSpec(memory_space=pltpu.VMEM)
ANY = pl.BlockSpec(memory_space=pl.ANY)


def call(kernel, name, outs, args, scratch=(), interpret=False):
    place = lambda x, near: pltpu.with_memory_space_constraint(x, pltpu.VMEM) if near else x
    kind = lambda near: pltpu.VMEM if near else jax.ShapeDtypeStruct
    if interpret:
        place, kind = (lambda x, near: x), (lambda near: jax.ShapeDtypeStruct)
    return pl.pallas_call(
        kernel,
        out_shape=tuple(kind(near)(shape, dtype) for (shape, dtype), near in outs),
        in_specs=[ANY if near is False else VMEM for _, near in args],
        out_specs=tuple(ANY if near is False else VMEM for _, near in outs),
        scratch_shapes=scratch,
        interpret=interpret,
        name=name,
    )(*[place(x, near) for x, near in args])


def local_outer(grad, mapping, feat_c, feat_e, **how):
    tile_i, tile_j, pair = grad.shape
    shape = (2 * tile_i * feat_c, tile_j * feat_e)
    grad = grad.reshape(tile_i * tile_j, pair)
    return call(
        functools.partial(outer_kernel, tile_i, tile_j, feat_e), "outer",
        [((shape, jnp.bfloat16), True)],
        [(grad, False), (mapping, False)],
        [
            pltpu.VMEM(grad.shape, grad.dtype), pltpu.VMEM(mapping.shape, mapping.dtype),
            pltpu.SemaphoreType.DMA((2,)),
        ],
        **how,
    )[0]


def local_left(total, gathered, block, outer, rows, **how):
    return call(
        functools.partial(left_kernel, total), "left", [(((rows, LANES), jnp.float32), True)],
        [(gathered, True), (block, True), (outer, True)], **how,
    )[0]


def local_right(total, seqs, gathered, outer, rows, block_rows, **how):
    f32 = jnp.float32
    return call(
        functools.partial(right_kernel, total, seqs), "right",
        [(((rows, LANES), f32), True), (((block_rows, LANES), f32), True)],
        [(gathered, True), (outer, True)], **how,
    )


def pack(left, right, count, **how):
    seqs, res, feat_c = left.shape
    feat_e = right.shape[2]
    rows = seqs * res * feat_c // LANES
    f32 = jnp.float32
    return call(
        functools.partial(pack_kernel, feat_c, feat_e), "pack",
        [(((rows, LANES), f32), True), (((count * rows, LANES), f32), True)],
        [(left.reshape(seqs * res, feat_c), None), (right.reshape(seqs * res, feat_e), None)],
        [pltpu.VMEM((seqs * feat_c, res), f32)], **how,
    )


def unpack(left_sum, right_parts, left, right, **how):
    seqs, res, feat_c = left.shape
    feat_e = right.shape[2]
    f32 = jnp.float32
    outs = call(
        functools.partial(unpack_kernel, feat_c, feat_e), "unpack",
        [(((seqs * res, feat_c), f32), None), (((seqs * res, feat_e), f32), None)],
        [(left_sum, True), (right_parts, True)],
        [pltpu.VMEM((seqs * feat_c, res), f32)], **how,
    )
    return outs[0].reshape(left.shape), outs[1].reshape(right.shape)


def pair_moves(rows, cols):
    half = cols // rows
    return [
        (r * cols + c, (c // half) * cols + (c % half) * rows + r)
        for r in range(rows)
        for c in range(cols)
    ]


def to_each(chunks, axis):
    chunks = chunks.reshape(lax.axis_size(axis), -1, LANES)
    return lax.all_to_all(chunks, axis, split_axis=0, concat_axis=0, tiled=True)


def on_device(left, right, grad, mapping):
    rows, cols = lax.axis_size("row"), lax.axis_size("col")
    seqs, res, feat_c = left.shape
    feat_e = right.shape[2]
    total = seqs * rows
    moves = pair_moves(rows, cols)
    back = [(b, a) for a, b in moves]
    both = ("row", "col")

    left_block, right_spread = pack(left, right, rows)
    block_rows = left_block.shape[0]
    left_block = lax.ppermute(left_block, both, moves)
    right_all = to_each(right_spread, "row").reshape(-1, LANES)
    outer = local_outer(grad, mapping, feat_c, feat_e)
    shared = local_left(total, right_all, left_block, outer, cols * 2 * block_rows)
    shared = to_each(shared, "col").reshape(-1, LANES)
    right_part, left_sum = local_right(
        total, seqs, shared, outer, right_spread.shape[0], block_rows
    )
    left_sum = lax.ppermute(left_sum, both, back)
    right_parts = to_each(right_part, "row").reshape(-1, LANES)
    return unpack(left_sum, right_parts, left, right)


def solution(mesh):
    spec = P("row", "col", None)
    return jax.shard_map(
        on_device,
        mesh=mesh,
        in_specs=(spec, spec, spec, P()),
        out_specs=(spec, spec),
        check_vma=False,
    )
```

```python
import functools
import itertools

import jax
import jax.numpy as jnp
import numpy as np
from jax import lax
from jax.experimental import pallas as pl
from jax.experimental.pallas import tpu as pltpu
from jax.sharding import PartitionSpec as P


LANES = 128
NT = (((1,), (1,)), ((), ()))
NN = (((1,), (0,)), ((), ()))


SIDES = (4, 2, 2, 8, 4)


def steps_along_y(far_z, turns_x):
    pick = jnp.where if isinstance(far_z, jax.Array) else lambda c, a, b: a if c else b
    near = pick(turns_x == 0, 4, pick(turns_x == 1, 3, pick(turns_x == 2, 6, 5)))
    far = pick(turns_x == 0, 2, pick(turns_x == 1, 1, pick(turns_x == 2, 0, 7)))
    return pick(far_z == 1, far, near)


def place_along_y(x, high, from_x, from_high):
    return (2 * x + high + steps_along_y(from_high ^ high, (from_x - x) % 4)) % 8


def pair_moves():
    pairs = []
    for from_x, from_high, from_core, y, z in itertools.product(*map(range, SIDES)):
        x, high, core, half = y // 2, y % 2, z // 2, z % 2
        to_y = place_along_y(x, high, from_x, from_high)
        source = np.ravel_multi_index((from_x, from_high, from_core, y, z), SIDES)
        target = np.ravel_multi_index((x, high, core, to_y, 2 * half + from_core), SIDES)
        pairs.append((int(source), int(target)))
    return pairs


def groups_along_y():
    row = lax.axis_index("row")
    x, high = row // 4, (row // 2) % 2
    return [place_along_y(x, high, from_x, from_high) for from_x in range(4) for from_high in range(2)]


def split(x):
    high = x.astype(jnp.bfloat16)
    return high, (x - high.astype(jnp.float32)).astype(jnp.bfloat16)


def product(a, b, dims):
    return lax.dot_general(a, b, dims, preferred_element_type=jnp.float32)


def swap_lane_groups(x):
    width = LANES // 4
    place = lax.broadcasted_iota(jnp.int32, x[0].shape, 1) // width
    front, even = place < 2, place % 2 == 0
    cross = (place == 0) | (place == 3)
    pick = jnp.where
    kept = pick(cross, x[0], x[2])
    turned = pltpu.roll(pick(cross, x[2], x[0]), 2 * width, 1)
    other = pltpu.roll(pick(front, x[3], x[1]), 2 * width, 1)
    firsts = (pick(front, kept, turned), pick(front, turned, kept))
    seconds = (pick(front, x[1], other), pick(front, other, x[3]))
    y = []
    for first, second in zip(firsts, seconds):
        turned = pltpu.roll(pick(even, second, first), width, 1)
        y += [pick(even, first, turned), pick(even, turned, second)]
    return y


def outer_kernel(
    tile_i, tile_j, feat_e, grad_hbm, map_hbm, out_ref, grad_ref, map_ref, in_sem
):
    group = LANES // feat_e
    part = tile_i // 2
    block = 2 * LANES
    steps = map_ref.shape[0] // block
    rows = out_ref.shape[0] // 4
    moved = [
        pltpu.make_async_copy(grad_hbm, grad_ref, in_sem.at[0]),
        pltpu.make_async_copy(map_hbm, map_ref, in_sem.at[1]),
    ]
    for copy in moved:
        copy.start()
    for copy in moved:
        copy.wait()
    grads = []
    for g in range(tile_j // group):
        grad = [grad_ref[pl.ds(g * group + j, tile_i, stride=tile_j), :] for j in range(group)]
        high, low = split(jnp.concatenate(grad, axis=0))
        grads.append((high, jnp.concatenate([high, low], axis=1)))
    for n in range(steps):
        map_high, map_low = split(map_ref[n * block : (n + 1) * block, :])
        map_both = jnp.concatenate([map_high, map_high], axis=1)
        for g, (grad_high, grad_both) in enumerate(grads):
            full = product(grad_both, map_both, NT) + product(grad_high, map_low, NT)
            for m in range(block // LANES):
                tiles = [
                    full[j * tile_i : (j + 1) * tile_i, m * LANES : (m + 1) * LANES]
                    for j in range(group)
                ]
                for k, tile in enumerate(swap_lane_groups(tiles)):
                    channel = (n * (block // LANES) + m) * group + k
                    for w, value in enumerate(split(tile)):
                        for h in range(2):
                            row = pl.ds((2 * w + h) * rows + channel * part, part)
                            lanes = pl.ds(g * LANES, LANES)
                            out_ref[row, lanes] = value[h * part : (h + 1) * part]


def load_rows(ref, first, total, pieces):
    return jnp.concatenate(
        [ref[pl.ds(first + p, total, stride=pieces), :] for p in range(pieces)], axis=1
    )


def left_kernel(total, groups, gathered_ref, block_ref, outer_ref, out_ref):
    steps = 4
    pieces = gathered_ref.shape[0] // total
    b_high, b_low = split(load_rows(gathered_ref, 0, total, pieces))
    b_both = jnp.concatenate([b_high, b_low], axis=0)
    turn = out_ref.shape[0] // (2 * total)
    pieces = turn // 2
    seqs = block_ref.shape[0] // pieces
    for p in range(pieces):
        mine = block_ref[pl.ds(p, seqs, stride=pieces), :]
        mine = jnp.concatenate([mine] * (total // seqs), axis=0)
        for h in range(2):
            out_ref[pl.ds(h * total * turn + p, total, stride=turn), :] = mine
    places = groups()
    tall = total // len(places)
    rows = outer_ref.shape[0] // 2
    span = rows // steps
    for n in range(steps):
        both = product(b_both, outer_ref[pl.ds(n * span, span), :], NT)
        last = product(b_high, outer_ref[pl.ds(rows + n * span, span), :], NT)
        left = both[:total] + both[total:] + last
        left = left * (1.0 / total)
        for m in range(span // LANES):
            h, p = divmod(n * (span // LANES) + m, pieces)
            for g, place in enumerate(places):
                row = pl.multiple_of(place * (2 * tall * turn), 2 * tall * turn) + h * tall * turn + pieces + p
                out_ref[pl.ds(row, tall, stride=turn), :] = left[
                    g * tall : (g + 1) * tall, m * LANES : (m + 1) * LANES
                ]


def right_kernel(total, seqs, groups, gathered_ref, outer_ref, out_ref, sum_ref):
    turn = gathered_ref.shape[0] // (2 * total)
    pieces = turn // 2
    places = groups()
    tall = total // len(places)

    def load(h, p):
        rows = [
            pl.multiple_of(place * (2 * tall * turn), 2 * tall * turn) + h * tall * turn + p
            for place in places
        ]
        return jnp.concatenate([gathered_ref[pl.ds(r, tall, stride=turn), :] for r in rows], axis=0)

    a_full = jnp.concatenate([load(h, p) for h in range(2) for p in range(pieces)], axis=1)
    a_high, a_low = split(a_full)
    rows = outer_ref.shape[0] // 2
    both = product(jnp.concatenate([a_high, a_low], axis=0), outer_ref[:rows, :], NN)
    right = both[:total] + both[total:] + product(a_high, outer_ref[rows:, :], NN)
    right = right * (1.0 / total)
    block = seqs * turn
    chunks = [gathered_ref[k : k + block, :] for k in range(0, gathered_ref.shape[0], block)]
    while len(chunks) > 1:
        chunks = [a + b for a, b in zip(chunks[::2], chunks[1::2])]
    for s in range(seqs):
        sum_ref[s * pieces : (s + 1) * pieces, :] = chunks[0][s * turn + pieces : (s + 1) * turn]
    pieces = out_ref.shape[0] // total
    for p in range(pieces):
        out_ref[pl.ds(p, total, stride=pieces), :] = right[:, p * LANES : (p + 1) * LANES]


def pack_kernel(feat_c, feat_e, left_ref, right_ref, block_ref, spread_ref, flat_ref):
    count = block_ref.shape[0]
    group = LANES // feat_e
    pieces = [right_ref[pl.ds(g, count, stride=group), :] for g in range(group)]
    mine = jnp.concatenate(pieces, axis=1)
    for k in range(spread_ref.shape[0] // count):
        spread_ref[k * count : (k + 1) * count, :] = mine
    res = LANES * count // flat_ref.shape[0]
    for s in range(left_ref.shape[0] // res):
        flat_ref[s * feat_c : (s + 1) * feat_c, :] = left_ref[s * res : (s + 1) * res, :].T
    group = LANES // res
    pieces = [flat_ref[pl.ds(g, count, stride=group), :] for g in range(group)]
    block_ref[...] = jnp.concatenate(pieces, axis=1)


def unpack_kernel(feat_c, feat_e, sum_ref, parts_ref, left_ref, right_ref, flat_ref):
    count = sum_ref.shape[0]
    res = LANES * count // flat_ref.shape[0]
    group = LANES // res
    for g in range(group):
        flat_ref[pl.ds(g, count, stride=group), :] = sum_ref[:, g * res : (g + 1) * res]
    for s in range(left_ref.shape[0] // res):
        left_ref[s * res : (s + 1) * res, :] = flat_ref[s * feat_c : (s + 1) * feat_c, :].T
    parts = [parts_ref[k : k + count, :] for k in range(0, parts_ref.shape[0], count)]
    while len(parts) > 1:
        parts = [a + b for a, b in zip(parts[::2], parts[1::2])]
    group = LANES // feat_e
    for g in range(group):
        right_ref[pl.ds(g, count, stride=group), :] = parts[0][:, g * feat_e : (g + 1) * feat_e]


VMEM = pl.BlockSpec(memory_space=pltpu.VMEM)
ANY = pl.BlockSpec(memory_space=pl.ANY)


def call(kernel, outs, args, scratch=(), interpret=False):
    place = lambda x, near: pltpu.with_memory_space_constraint(x, pltpu.VMEM) if near else x
    kind = lambda near: pltpu.VMEM if near else jax.ShapeDtypeStruct
    if interpret:
        place, kind = (lambda x, near: x), (lambda near: jax.ShapeDtypeStruct)
    return pl.pallas_call(
        kernel,
        out_shape=tuple(kind(near)(shape, dtype) for (shape, dtype), near in outs),
        in_specs=[ANY if near is False else VMEM for _, near in args],
        out_specs=tuple(ANY if near is False else VMEM for _, near in outs),
        scratch_shapes=scratch,
        interpret=interpret,
    )(*[place(x, near) for x, near in args])


def local_outer(grad, mapping, feat_c, feat_e, **how):
    tile_i, tile_j, pair = grad.shape
    shape = (2 * tile_i * feat_c, tile_j * feat_e)
    grad = grad.reshape(tile_i * tile_j, pair)
    return call(
        functools.partial(outer_kernel, tile_i, tile_j, feat_e),
        [((shape, jnp.bfloat16), True)],
        [(grad, False), (mapping, False)],
        [
            pltpu.VMEM(grad.shape, grad.dtype), pltpu.VMEM(mapping.shape, mapping.dtype),
            pltpu.SemaphoreType.DMA((2,)),
        ],
        **how,
    )[0]


def local_left(total, gathered, block, outer, rows, groups=groups_along_y, **how):
    return call(
        functools.partial(left_kernel, total, groups), [(((rows, LANES), jnp.float32), True)],
        [(gathered, True), (block, True), (outer, True)], **how,
    )[0]


def local_right(total, seqs, gathered, outer, rows, block_rows, groups=groups_along_y, **how):
    f32 = jnp.float32
    return call(
        functools.partial(right_kernel, total, seqs, groups),
        [(((rows, LANES), f32), True), (((block_rows, LANES), f32), True)],
        [(gathered, True), (outer, True)], **how,
    )


def pack(left, right, count, **how):
    seqs, res, feat_c = left.shape
    feat_e = right.shape[2]
    rows = seqs * res * feat_c // LANES
    f32 = jnp.float32
    return call(
        functools.partial(pack_kernel, feat_c, feat_e),
        [(((rows, LANES), f32), True), (((count * rows, LANES), f32), True)],
        [(left.reshape(seqs * res, feat_c), None), (right.reshape(seqs * res, feat_e), None)],
        [pltpu.VMEM((seqs * feat_c, res), f32)], **how,
    )


def unpack(left_sum, right_parts, left, right, **how):
    seqs, res, feat_c = left.shape
    feat_e = right.shape[2]
    f32 = jnp.float32
    outs = call(
        functools.partial(unpack_kernel, feat_c, feat_e),
        [(((seqs * res, feat_c), f32), None), (((seqs * res, feat_e), f32), None)],
        [(left_sum, True), (right_parts, True)],
        [pltpu.VMEM((seqs * feat_c, res), f32)], **how,
    )
    return outs[0].reshape(left.shape), outs[1].reshape(right.shape)


def to_each(chunks, axis):
    chunks = chunks.reshape(lax.axis_size(axis), -1, LANES)
    return lax.all_to_all(chunks, axis, split_axis=0, concat_axis=0, tiled=True)


def compute(left, right, grad, mapping):
    rows, cols = lax.axis_size("row"), lax.axis_size("col")
    seqs, _, feat_c = left.shape
    feat_e = right.shape[2]
    total = seqs * rows
    moves = pair_moves()
    back = [(b, a) for a, b in moves]
    both = ("row", "col")

    left_block, right_spread = pack(left, right, rows)
    block_rows = left_block.shape[0]
    left_block = lax.ppermute(left_block, both, moves)
    right_all = to_each(right_spread, "row").reshape(-1, LANES)
    outer = local_outer(grad, mapping, feat_c, feat_e)
    shared = local_left(total, right_all, left_block, outer, cols * 2 * block_rows)
    shared = to_each(shared, "col").reshape(-1, LANES)
    right_part, left_sum = local_right(
        total, seqs, shared, outer, right_spread.shape[0], block_rows
    )
    left_sum = lax.ppermute(left_sum, both, back)
    right_parts = to_each(right_part, "row").reshape(-1, LANES)
    return unpack(left_sum, right_parts, left, right)


def solution(mesh):
    spec = P("row", "col", None)
    return jax.shard_map(
        compute,
        mesh=mesh,
        in_specs=(spec, spec, spec, P()),
        out_specs=(spec, spec),
        check_vma=False,
    )
```

```python
import functools
import itertools

import jax
import jax.numpy as jnp
import numpy as np
from jax import lax
from jax.experimental import pallas as pl
from jax.experimental.pallas import tpu as pltpu
from jax.sharding import Mesh
from jax.sharding import PartitionSpec as P


LANES = 128
NT = (((1,), (1,)), ((), ()))
NN = (((1,), (0,)), ((), ()))


SIDES = {"x": 4, "high": 2, "core": 2, "y": 8, "low": 4}
ALL = tuple(SIDES)
ROW = ("core", "x", "high")
NEAR = ("core", "x")
COL = ("low", "y")


def steps_along_y(far_z, turns_x):
    pick = jnp.where if isinstance(turns_x, jax.Array) else lambda c, a, b: a if c else b
    near = pick(turns_x == 0, 4, pick(turns_x == 1, 3, pick(turns_x == 2, 6, 5)))
    far = pick(turns_x == 0, 2, pick(turns_x == 1, 1, pick(turns_x == 2, 0, 7)))
    return pick(far_z == 1, far, near)


def place_along_y(x, high, from_x, other):
    return (2 * x + high + steps_along_y(other, (from_x - x) % 4)) % 8


def pair_moves():
    pairs = []
    for from_x, from_high, from_core, y, z in itertools.product(*map(range, SIDES.values())):
        x, high, core, half = y // 2, y % 2, z // 2, z % 2
        to_y = place_along_y(x, high, from_x, from_high ^ high)
        source = np.ravel_multi_index((from_x, from_high, from_core, y, z), tuple(SIDES.values()))
        target = np.ravel_multi_index((x, high, core, to_y, 2 * half + from_core), tuple(SIDES.values()))
        pairs.append((int(source), int(target)))
    return pairs


def column_places():
    x, high = lax.axis_index("x"), lax.axis_index("high")
    return [
        [
            (2 * half + core) * SIDES["y"] + place_along_y(x, high, from_x, other)
            for core in range(2)
            for from_x in range(4)
            for other in range(2)
        ]
        for half in range(2)
    ]


def row_places():
    high = lax.axis_index("high")
    return [
        (core * 4 + to_x) * 2 + (1 - high if other else high)
        for core in range(2)
        for to_x in range(4)
        for other in range(2)
    ]


def split(x):
    high = x.astype(jnp.bfloat16)
    return high, (x - high.astype(jnp.float32)).astype(jnp.bfloat16)


def product(a, b, dims):
    return lax.dot_general(a, b, dims, preferred_element_type=jnp.float32)


def swap_lane_groups(x):
    width = LANES // 4
    place = lax.broadcasted_iota(jnp.int32, x[0].shape, 1) // width
    front, even = place < 2, place % 2 == 0
    cross = (place == 0) | (place == 3)
    pick = jnp.where
    kept = pick(cross, x[0], x[2])
    turned = pltpu.roll(pick(cross, x[2], x[0]), 2 * width, 1)
    other = pltpu.roll(pick(front, x[3], x[1]), 2 * width, 1)
    firsts = (pick(front, kept, turned), pick(front, turned, kept))
    seconds = (pick(front, x[1], other), pick(front, other, x[3]))
    y = []
    for first, second in zip(firsts, seconds):
        turned = pltpu.roll(pick(even, second, first), width, 1)
        y += [pick(even, first, turned), pick(even, turned, second)]
    return y


def outer_kernel(
    tile_i, tile_j, feat_e, grad_hbm, map_hbm, out_ref, grad_ref, map_ref, in_sem
):
    group = LANES // feat_e
    part = tile_i // 2
    block = 2 * LANES
    steps = map_ref.shape[0] // block
    rows = out_ref.shape[0] // 4
    moved = [
        pltpu.make_async_copy(grad_hbm, grad_ref, in_sem.at[0]),
        pltpu.make_async_copy(map_hbm, map_ref, in_sem.at[1]),
    ]
    for copy in moved:
        copy.start()
    for copy in moved:
        copy.wait()
    grads = []
    for g in range(tile_j // group):
        grad = [grad_ref[pl.ds(g * group + j, tile_i, stride=tile_j), :] for j in range(group)]
        high, low = split(jnp.concatenate(grad, axis=0))
        grads.append((high, jnp.concatenate([high, low], axis=1)))
    for n in range(steps):
        map_high, map_low = split(map_ref[n * block : (n + 1) * block, :])
        map_both = jnp.concatenate([map_high, map_high], axis=1)
        for g, (grad_high, grad_both) in enumerate(grads):
            full = product(grad_both, map_both, NT) + product(grad_high, map_low, NT)
            for m in range(block // LANES):
                tiles = [
                    full[j * tile_i : (j + 1) * tile_i, m * LANES : (m + 1) * LANES]
                    for j in range(group)
                ]
                for k, tile in enumerate(swap_lane_groups(tiles)):
                    channel = (n * (block // LANES) + m) * group + k
                    for w, value in enumerate(split(tile)):
                        for h in range(2):
                            row = pl.ds((2 * w + h) * rows + channel * part, part)
                            lanes = pl.ds(g * LANES, LANES)
                            out_ref[row, lanes] = value[h * part : (h + 1) * part]


def load_rows(ref, first, total, pieces):
    return jnp.concatenate(
        [ref[pl.ds(first + p, total, stride=pieces), :] for p in range(pieces)], axis=1
    )


def left_kernel(total, places, gathered_ref, block_ref, outer_ref, out_ref):
    steps = 4
    pieces = gathered_ref.shape[0] // total
    b_high, b_low = split(load_rows(gathered_ref, 0, total, pieces))
    b_both = jnp.concatenate([b_high, b_low], axis=0)
    turn = out_ref.shape[0] // (2 * total)
    pieces = turn // 2
    seqs = block_ref.shape[0] // pieces
    for p in range(pieces):
        mine = block_ref[pl.ds(p, seqs, stride=pieces), :]
        mine = jnp.concatenate([mine] * (total // seqs), axis=0)
        for h in range(2):
            out_ref[pl.ds(h * total * turn + p, total, stride=turn), :] = mine
    places = places()
    block = seqs * turn
    rows = outer_ref.shape[0] // 2
    span = rows // steps
    for n in range(steps):
        both = product(b_both, outer_ref[pl.ds(n * span, span), :], NT)
        last = product(b_high, outer_ref[pl.ds(rows + n * span, span), :], NT)
        left = both[:total] + both[total:] + last
        left = left * (1.0 / total)
        for m in range(span // LANES):
            h, p = divmod(n * (span // LANES) + m, pieces)
            for k, place in enumerate(places[h]):
                row = pl.multiple_of(place * block, block) + pieces + p
                out_ref[pl.ds(row, seqs, stride=turn), :] = left[
                    k * seqs : (k + 1) * seqs, m * LANES : (m + 1) * LANES
                ]


def right_kernel(total, seqs, places, row_places, gathered_ref, outer_ref, out_ref, sum_ref):
    turn = gathered_ref.shape[0] // (2 * total)
    pieces = turn // 2
    places = places()
    block = seqs * turn

    def load(h, p):
        rows = [pl.multiple_of(place * block, block) + p for place in places[h]]
        return jnp.concatenate([gathered_ref[pl.ds(r, seqs, stride=turn), :] for r in rows], axis=0)

    a_full = jnp.concatenate([load(h, p) for h in range(2) for p in range(pieces)], axis=1)
    a_high, a_low = split(a_full)
    rows = outer_ref.shape[0] // 2
    both = product(jnp.concatenate([a_high, a_low], axis=0), outer_ref[:rows, :], NN)
    right = both[:total] + both[total:] + product(a_high, outer_ref[rows:, :], NN)
    right = right * (1.0 / total)
    chunks = [gathered_ref[k : k + block, :] for k in range(0, gathered_ref.shape[0], block)]
    while len(chunks) > 1:
        chunks = [a + b for a, b in zip(chunks[::2], chunks[1::2])]
    for s in range(seqs):
        sum_ref[s * pieces : (s + 1) * pieces, :] = chunks[0][s * turn + pieces : (s + 1) * turn]
    pieces = out_ref.shape[0] // total
    block = seqs * pieces
    for k, place in enumerate(row_places()):
        for p in range(pieces):
            row = pl.multiple_of(place * block, block) + p
            out_ref[pl.ds(row, seqs, stride=pieces), :] = right[
                k * seqs : (k + 1) * seqs, p * LANES : (p + 1) * LANES
            ]


def pack_kernel(feat_c, feat_e, left_ref, right_ref, block_ref, spread_ref, flat_ref):
    count = block_ref.shape[0]
    group = LANES // feat_e
    pieces = [right_ref[pl.ds(g, count, stride=group), :] for g in range(group)]
    mine = jnp.concatenate(pieces, axis=1)
    for k in range(spread_ref.shape[0] // count):
        spread_ref[k * count : (k + 1) * count, :] = mine
    res = LANES * count // flat_ref.shape[0]
    for s in range(left_ref.shape[0] // res):
        flat_ref[s * feat_c : (s + 1) * feat_c, :] = left_ref[s * res : (s + 1) * res, :].T
    group = LANES // res
    pieces = [flat_ref[pl.ds(g, count, stride=group), :] for g in range(group)]
    block_ref[...] = jnp.concatenate(pieces, axis=1)


def unpack_kernel(feat_c, feat_e, sum_ref, parts_ref, left_ref, right_ref, flat_ref):
    count = sum_ref.shape[0]
    res = LANES * count // flat_ref.shape[0]
    group = LANES // res
    for g in range(group):
        flat_ref[pl.ds(g, count, stride=group), :] = sum_ref[:, g * res : (g + 1) * res]
    for s in range(left_ref.shape[0] // res):
        left_ref[s * res : (s + 1) * res, :] = flat_ref[s * feat_c : (s + 1) * feat_c, :].T
    parts = [parts_ref[k : k + count, :] for k in range(0, parts_ref.shape[0], count)]
    while len(parts) > 1:
        parts = [a + b for a, b in zip(parts[::2], parts[1::2])]
    group = LANES // feat_e
    for g in range(group):
        right_ref[pl.ds(g, count, stride=group), :] = parts[0][:, g * feat_e : (g + 1) * feat_e]


VMEM = pl.BlockSpec(memory_space=pltpu.VMEM)
ANY = pl.BlockSpec(memory_space=pl.ANY)


def call(kernel, outs, args, scratch=(), interpret=False):
    place = lambda x, near: pltpu.with_memory_space_constraint(x, pltpu.VMEM) if near else x
    kind = lambda near: pltpu.VMEM if near else jax.ShapeDtypeStruct
    if interpret:
        place, kind = (lambda x, near: x), (lambda near: jax.ShapeDtypeStruct)
    return pl.pallas_call(
        kernel,
        out_shape=tuple(kind(near)(shape, dtype) for (shape, dtype), near in outs),
        in_specs=[ANY if near is False else VMEM for _, near in args],
        out_specs=tuple(ANY if near is False else VMEM for _, near in outs),
        scratch_shapes=scratch,
        interpret=interpret,
    )(*[place(x, near) for x, near in args])


def local_outer(grad, mapping, feat_c, feat_e, **how):
    tile_i, tile_j, pair = grad.shape
    shape = (2 * tile_i * feat_c, tile_j * feat_e)
    grad = grad.reshape(tile_i * tile_j, pair)
    return call(
        functools.partial(outer_kernel, tile_i, tile_j, feat_e),
        [((shape, jnp.bfloat16), True)],
        [(grad, False), (mapping, False)],
        [
            pltpu.VMEM(grad.shape, grad.dtype), pltpu.VMEM(mapping.shape, mapping.dtype),
            pltpu.SemaphoreType.DMA((2,)),
        ],
        **how,
    )[0]


def local_left(total, gathered, block, outer, rows, places=column_places, **how):
    return call(
        functools.partial(left_kernel, total, places), [(((rows, LANES), jnp.float32), True)],
        [(gathered, True), (block, True), (outer, True)], **how,
    )[0]


def local_right(total, seqs, gathered, outer, rows, block_rows, places=column_places, row_places=row_places, **how):
    f32 = jnp.float32
    return call(
        functools.partial(right_kernel, total, seqs, places, row_places),
        [(((rows, LANES), f32), True), (((block_rows, LANES), f32), True)],
        [(gathered, True), (outer, True)], **how,
    )


def pack(left, right, count, **how):
    seqs, res, feat_c = left.shape
    feat_e = right.shape[2]
    rows = seqs * res * feat_c // LANES
    f32 = jnp.float32
    return call(
        functools.partial(pack_kernel, feat_c, feat_e),
        [(((rows, LANES), f32), True), (((count * rows, LANES), f32), True)],
        [(left.reshape(seqs * res, feat_c), None), (right.reshape(seqs * res, feat_e), None)],
        [pltpu.VMEM((seqs * feat_c, res), f32)], **how,
    )


def unpack(left_sum, right_parts, left, right, **how):
    seqs, res, feat_c = left.shape
    feat_e = right.shape[2]
    f32 = jnp.float32
    outs = call(
        functools.partial(unpack_kernel, feat_c, feat_e),
        [(((seqs * res, feat_c), f32), None), (((seqs * res, feat_e), f32), None)],
        [(left_sum, True), (right_parts, True)],
        [pltpu.VMEM((seqs * feat_c, res), f32)], **how,
    )
    return outs[0].reshape(left.shape), outs[1].reshape(right.shape)


def to_each(chunks, axis):
    chunks = chunks.reshape(lax.axis_size(axis), -1, LANES)
    return lax.all_to_all(chunks, axis, split_axis=0, concat_axis=0, tiled=True)


def compute(left, right, grad, mapping):
    rows, cols = lax.axis_size(ROW), lax.axis_size(COL)
    seqs, _, feat_c = left.shape
    feat_e = right.shape[2]
    total = seqs * rows
    moves = pair_moves()
    back = [(b, a) for a, b in moves]

    left_block, right_block = pack(left, right, 1)
    block_rows = left_block.shape[0]
    across = lax.ppermute(right_block, "high", [(0, 1), (1, 0)])
    left_block = lax.ppermute(left_block, ALL, moves)
    near = lax.axis_size(NEAR)
    spread = jnp.broadcast_to(jnp.concatenate([right_block, across])[None], (near, 2 * block_rows, LANES))
    right_all = to_each(spread, NEAR).reshape(-1, LANES)
    outer = local_outer(grad, mapping, feat_c, feat_e)
    shared = local_left(total, right_all, left_block, outer, cols * 2 * block_rows)
    shared = to_each(shared, COL).reshape(-1, LANES)
    right_part, left_sum = local_right(
        total, seqs, shared, outer, rows * block_rows, block_rows
    )
    left_sum = lax.ppermute(left_sum, ALL, back)
    right_parts = to_each(right_part, ROW).reshape(-1, LANES)
    return unpack(left_sum, right_parts, left, right)


def solution(mesh):
    mesh = Mesh(mesh.devices.reshape(tuple(SIDES.values())), ALL)
    spec = P(ALL[:3], ALL[3:], None)
    return jax.shard_map(
        compute,
        mesh=mesh,
        in_specs=(spec, spec, spec, P()),
        out_specs=(spec, spec),
        check_vma=False,
    )
```

```python
import functools
import itertools

import jax
import jax.numpy as jnp
import numpy as np
from jax import lax
from jax.experimental import pallas as pl
from jax.experimental.pallas import tpu as pltpu
from jax.sharding import Mesh
from jax.sharding import PartitionSpec as P


LANES = 128
NT = (((1,), (1,)), ((), ()))
NN = (((1,), (0,)), ((), ()))


SIDES = {"x": 4, "high": 2, "core": 2, "y": 8, "low": 4}
ALL = tuple(SIDES)
ROW = ("core", "x", "high")
NEAR = ("core", "x")
COL = ("low", "y")


def steps_along_y(far_z, turns_x):
    pick = jnp.where if isinstance(turns_x, jax.Array) else lambda c, a, b: a if c else b
    near = pick(turns_x == 0, 4, pick(turns_x == 1, 3, pick(turns_x == 2, 6, 5)))
    far = pick(turns_x == 0, 2, pick(turns_x == 1, 1, pick(turns_x == 2, 0, 7)))
    return pick(far_z == 1, far, near)


def place_along_y(x, high, from_x, other):
    return (2 * x + high + steps_along_y(other, (from_x - x) % 4)) % 8


def pair_moves():
    pairs = []
    for from_x, from_high, from_core, y, z in itertools.product(*map(range, SIDES.values())):
        x, high, core, half = y // 2, y % 2, z // 2, z % 2
        to_y = place_along_y(x, high, from_x, from_high ^ high)
        source = np.ravel_multi_index((from_x, from_high, from_core, y, z), tuple(SIDES.values()))
        target = np.ravel_multi_index((x, high, core, to_y, 2 * half + from_core), tuple(SIDES.values()))
        pairs.append((int(source), int(target)))
    return pairs


def column_places():
    x, high = lax.axis_index("x"), lax.axis_index("high")
    return [
        [
            (2 * half + core) * SIDES["y"] + place_along_y(x, high, from_x, other)
            for core in range(2)
            for from_x in range(4)
            for other in range(2)
        ]
        for half in range(2)
    ]


def row_places():
    high = lax.axis_index("high")
    return [
        (core * 4 + to_x) * 2 + (1 - high if other else high)
        for core in range(2)
        for to_x in range(4)
        for other in range(2)
    ]


def split(x):
    high = x.astype(jnp.bfloat16)
    return high, (x - high.astype(jnp.float32)).astype(jnp.bfloat16)


def product(a, b, dims):
    return lax.dot_general(a, b, dims, preferred_element_type=jnp.float32)


def swap_lane_groups(x):
    width = LANES // 4
    place = lax.broadcasted_iota(jnp.int32, x[0].shape, 1) // width
    front, even = place < 2, place % 2 == 0
    cross = (place == 0) | (place == 3)
    pick = jnp.where
    kept = pick(cross, x[0], x[2])
    turned = pltpu.roll(pick(cross, x[2], x[0]), 2 * width, 1)
    other = pltpu.roll(pick(front, x[3], x[1]), 2 * width, 1)
    firsts = (pick(front, kept, turned), pick(front, turned, kept))
    seconds = (pick(front, x[1], other), pick(front, other, x[3]))
    y = []
    for first, second in zip(firsts, seconds):
        turned = pltpu.roll(pick(even, second, first), width, 1)
        y += [pick(even, first, turned), pick(even, turned, second)]
    return y


def outer_kernel(
    tile_i, tile_j, feat_e, grad_hbm, map_hbm, out_ref, grad_ref, map_ref, in_sem
):
    group = LANES // feat_e
    part = tile_i // 2
    block = 2 * LANES
    steps = map_ref.shape[0] // block
    rows = out_ref.shape[0] // 4
    moved = [
        pltpu.make_async_copy(grad_hbm, grad_ref, in_sem.at[0]),
        pltpu.make_async_copy(map_hbm, map_ref, in_sem.at[1]),
    ]
    for copy in moved:
        copy.start()
    for copy in moved:
        copy.wait()
    grads = []
    for g in range(tile_j // group):
        grad = [grad_ref[pl.ds(g * group + j, tile_i, stride=tile_j), :] for j in range(group)]
        high, low = split(jnp.concatenate(grad, axis=0))
        grads.append((high, jnp.concatenate([high, low], axis=1)))
    for n in range(steps):
        map_high, map_low = split(map_ref[n * block : (n + 1) * block, :])
        map_both = jnp.concatenate([map_high, map_high], axis=1)
        for g, (grad_high, grad_both) in enumerate(grads):
            full = product(grad_both, map_both, NT) + product(grad_high, map_low, NT)
            for m in range(block // LANES):
                tiles = [
                    full[j * tile_i : (j + 1) * tile_i, m * LANES : (m + 1) * LANES]
                    for j in range(group)
                ]
                for k, tile in enumerate(swap_lane_groups(tiles)):
                    channel = (n * (block // LANES) + m) * group + k
                    for w, value in enumerate(split(tile)):
                        for h in range(2):
                            row = pl.ds((2 * w + h) * rows + channel * part, part)
                            lanes = pl.ds(g * LANES, LANES)
                            out_ref[row, lanes] = value[h * part : (h + 1) * part]


def load_rows(ref, first, total, pieces):
    return jnp.concatenate(
        [ref[pl.ds(first + p, total, stride=pieces), :] for p in range(pieces)], axis=1
    )


def left_kernel(total, places, gathered_ref, block_ref, outer_ref, out_ref):
    steps = 4
    pieces = gathered_ref.shape[0] // total
    b_high, b_low = split(load_rows(gathered_ref, 0, total, pieces))
    b_both = jnp.concatenate([b_high, b_low], axis=0)
    turn = out_ref.shape[0] // (2 * total)
    pieces = turn // 2
    seqs = block_ref.shape[0] // pieces
    for p in range(pieces):
        mine = block_ref[pl.ds(p, seqs, stride=pieces), :]
        mine = jnp.concatenate([mine] * (total // seqs), axis=0)
        for h in range(2):
            out_ref[pl.ds(h * total * turn + p, total, stride=turn), :] = mine
    places = places()
    block = seqs * turn
    rows = outer_ref.shape[0] // 2
    span = rows // steps
    for n in range(steps):
        both = product(b_both, outer_ref[pl.ds(n * span, span), :], NT)
        last = product(b_high, outer_ref[pl.ds(rows + n * span, span), :], NT)
        left = both[:total] + both[total:] + last
        left = left * (1.0 / total)
        for m in range(span // LANES):
            h, p = divmod(n * (span // LANES) + m, pieces)
            for k, place in enumerate(places[h]):
                row = pl.multiple_of(place * block, block) + pieces + p
                out_ref[pl.ds(row, seqs, stride=turn), :] = left[
                    k * seqs : (k + 1) * seqs, m * LANES : (m + 1) * LANES
                ]


def right_kernel(total, seqs, places, row_places, gathered_ref, outer_ref, out_ref, sum_ref):
    turn = gathered_ref.shape[0] // (2 * total)
    pieces = turn // 2
    places = places()
    block = seqs * turn

    def load(h, p):
        rows = [pl.multiple_of(place * block, block) + p for place in places[h]]
        return jnp.concatenate([gathered_ref[pl.ds(r, seqs, stride=turn), :] for r in rows], axis=0)

    a_full = jnp.concatenate([load(h, p) for h in range(2) for p in range(pieces)], axis=1)
    a_high, a_low = split(a_full)
    rows = outer_ref.shape[0] // 2
    both = product(jnp.concatenate([a_high, a_low], axis=0), outer_ref[:rows, :], NN)
    right = both[:total] + both[total:] + product(a_high, outer_ref[rows:, :], NN)
    right = right * (1.0 / total)
    chunks = [gathered_ref[k : k + block, :] for k in range(0, gathered_ref.shape[0], block)]
    while len(chunks) > 1:
        chunks = [a + b for a, b in zip(chunks[::2], chunks[1::2])]
    for s in range(seqs):
        sum_ref[s * pieces : (s + 1) * pieces, :] = chunks[0][s * turn + pieces : (s + 1) * turn]
    pieces = out_ref.shape[0] // total
    block = seqs * pieces
    for k, place in enumerate(row_places()):
        for p in range(pieces):
            row = pl.multiple_of(place * block, block) + p
            out_ref[pl.ds(row, seqs, stride=pieces), :] = right[
                k * seqs : (k + 1) * seqs, p * LANES : (p + 1) * LANES
            ]


def pack_kernel(feat_c, feat_e, left_ref, right_ref, block_ref, spread_ref, flat_ref):
    count = block_ref.shape[0]
    group = LANES // feat_e
    pieces = [right_ref[pl.ds(g, count, stride=group), :] for g in range(group)]
    mine = jnp.concatenate(pieces, axis=1)
    for k in range(spread_ref.shape[0] // count):
        spread_ref[k * count : (k + 1) * count, :] = mine
    res = LANES * count // flat_ref.shape[0]
    for s in range(left_ref.shape[0] // res):
        flat_ref[s * feat_c : (s + 1) * feat_c, :] = left_ref[s * res : (s + 1) * res, :].T
    group = LANES // res
    pieces = [flat_ref[pl.ds(g, count, stride=group), :] for g in range(group)]
    block_ref[...] = jnp.concatenate(pieces, axis=1)


def unpack_left_kernel(feat_c, sum_ref, left_ref, flat_ref):
    count = sum_ref.shape[0]
    res = LANES * count // flat_ref.shape[0]
    group = LANES // res
    for g in range(group):
        flat_ref[pl.ds(g, count, stride=group), :] = sum_ref[:, g * res : (g + 1) * res]
    for s in range(left_ref.shape[0] // res):
        left_ref[s * res : (s + 1) * res, :] = flat_ref[s * feat_c : (s + 1) * feat_c, :].T


def unpack_right_kernel(feat_e, parts_ref, right_ref):
    count = right_ref.shape[0] * feat_e // LANES
    parts = [parts_ref[k : k + count, :] for k in range(0, parts_ref.shape[0], count)]
    while len(parts) > 1:
        parts = [a + b for a, b in zip(parts[::2], parts[1::2])]
    group = LANES // feat_e
    for g in range(group):
        right_ref[pl.ds(g, count, stride=group), :] = parts[0][:, g * feat_e : (g + 1) * feat_e]


VMEM = pl.BlockSpec(memory_space=pltpu.VMEM)
ANY = pl.BlockSpec(memory_space=pl.ANY)


def call(kernel, outs, args, scratch=(), interpret=False):
    place = lambda x, near: pltpu.with_memory_space_constraint(x, pltpu.VMEM) if near else x
    kind = lambda near: pltpu.VMEM if near else jax.ShapeDtypeStruct
    if interpret:
        place, kind = (lambda x, near: x), (lambda near: jax.ShapeDtypeStruct)
    return pl.pallas_call(
        kernel,
        out_shape=tuple(kind(near)(shape, dtype) for (shape, dtype), near in outs),
        in_specs=[ANY if near is False else VMEM for _, near in args],
        out_specs=tuple(ANY if near is False else VMEM for _, near in outs),
        scratch_shapes=scratch,
        interpret=interpret,
    )(*[place(x, near) for x, near in args])


def local_outer(grad, mapping, feat_c, feat_e, **how):
    tile_i, tile_j, pair = grad.shape
    shape = (2 * tile_i * feat_c, tile_j * feat_e)
    grad = grad.reshape(tile_i * tile_j, pair)
    return call(
        functools.partial(outer_kernel, tile_i, tile_j, feat_e),
        [((shape, jnp.bfloat16), True)],
        [(grad, False), (mapping, False)],
        [
            pltpu.VMEM(grad.shape, grad.dtype), pltpu.VMEM(mapping.shape, mapping.dtype),
            pltpu.SemaphoreType.DMA((2,)),
        ],
        **how,
    )[0]


def local_left(total, gathered, block, outer, rows, places=column_places, **how):
    return call(
        functools.partial(left_kernel, total, places), [(((rows, LANES), jnp.float32), True)],
        [(gathered, True), (block, True), (outer, True)], **how,
    )[0]


def local_right(total, seqs, gathered, outer, rows, block_rows, places=column_places, row_places=row_places, **how):
    f32 = jnp.float32
    return call(
        functools.partial(right_kernel, total, seqs, places, row_places),
        [(((rows, LANES), f32), True), (((block_rows, LANES), f32), True)],
        [(gathered, True), (outer, True)], **how,
    )


def pack(left, right, count, **how):
    seqs, res, feat_c = left.shape
    feat_e = right.shape[2]
    rows = seqs * res * feat_c // LANES
    f32 = jnp.float32
    return call(
        functools.partial(pack_kernel, feat_c, feat_e),
        [(((rows, LANES), f32), True), (((count * rows, LANES), f32), True)],
        [(left.reshape(seqs * res, feat_c), None), (right.reshape(seqs * res, feat_e), None)],
        [pltpu.VMEM((seqs * feat_c, res), f32)], **how,
    )


def unpack_left(left_sum, left, **how):
    seqs, res, feat_c = left.shape
    out = call(
        functools.partial(unpack_left_kernel, feat_c),
        [(((seqs * res, feat_c), jnp.float32), None)], [(left_sum, True)],
        [pltpu.VMEM((seqs * feat_c, res), jnp.float32)], **how,
    )[0]
    return out.reshape(left.shape)


def unpack_right(right_parts, right, **how):
    seqs, res, feat_e = right.shape
    out = call(
        functools.partial(unpack_right_kernel, feat_e),
        [(((seqs * res, feat_e), jnp.float32), None)], [(right_parts, True)], **how,
    )[0]
    return out.reshape(right.shape)


def to_each(chunks, axis):
    chunks = chunks.reshape(lax.axis_size(axis), -1, LANES)
    return lax.all_to_all(chunks, axis, split_axis=0, concat_axis=0, tiled=True)


def compute(left, right, grad, mapping):
    rows, cols = lax.axis_size(ROW), lax.axis_size(COL)
    seqs, _, feat_c = left.shape
    feat_e = right.shape[2]
    total = seqs * rows
    moves = pair_moves()
    back = [(b, a) for a, b in moves]

    left_block, right_block = pack(left, right, 1)
    block_rows = left_block.shape[0]
    across = lax.ppermute(right_block, "high", [(0, 1), (1, 0)])
    left_block = lax.ppermute(left_block, ALL, moves)
    near = lax.axis_size(NEAR)
    spread = jnp.broadcast_to(jnp.concatenate([right_block, across])[None], (near, 2 * block_rows, LANES))
    right_all = to_each(spread, NEAR).reshape(-1, LANES)
    outer = local_outer(grad, mapping, feat_c, feat_e)
    shared = local_left(total, right_all, left_block, outer, cols * 2 * block_rows)
    shared = to_each(shared, COL).reshape(-1, LANES)
    right_part, left_sum = local_right(
        total, seqs, shared, outer, rows * block_rows, block_rows
    )
    left_sum = lax.ppermute(left_sum, ALL, back)
    right_parts = to_each(right_part, ROW).reshape(-1, LANES)
    grad_right = unpack_right(right_parts, right)
    return unpack_left(left_sum, left), grad_right


def solution(mesh):
    mesh = Mesh(mesh.devices.reshape(tuple(SIDES.values())), ALL)
    spec = P(ALL[:3], ALL[3:], None)
    return jax.shard_map(
        compute,
        mesh=mesh,
        in_specs=(spec, spec, spec, P()),
        out_specs=(spec, spec),
        check_vma=False,
    )
```
